256 devices in a mesh: rep: 16 (over y, x), fsdp: 16 (over z, core).
Axes of the slice: x: 4, y: 4, z: 8, core: 2. Of those that a mesh axis runs over, the one named last changes fastest.
Arguments:
- hidden_acts: bfloat16 [16, 8192, 512], P('rep', 'fsdp'), may hold values from -6 to 6
- out_grads: bfloat16 [16, 8192, 8192], P('rep', 'fsdp'), may hold values from -0.15625 to 0.15625
- anchor: float32 [512, 8192], P('fsdp'), may hold values from -6 to 6
- drift: float32 [16, 512, 8192], P('rep', 'fsdp'), may hold values from -120 to 120, as said below
- adam_first: float32 [16, 512, 8192], P('rep', 'fsdp'), may hold values from -6 to 6
- adam_second: float32 [16, 512, 8192], P('rep', 'fsdp'), may hold values from 0.3 to 3
- outer_momentum: float32 [512, 8192], P('fsdp'), may hold values from -6 to 6
Outputs:
- new_first: float32 [16, 512, 8192], P('rep', 'fsdp')
- new_second: float32 [16, 512, 8192], P('rep', 'fsdp')
- new_momentum: float32 [512, 8192], P('fsdp')
- new_anchor: float32 [512, 8192], P('fsdp')
The draws below stay inside these ranges and needn't reach their ends.
Inputs may be any that keep to these rules, and one draw needn't show every extreme that they name: drift entries are finite reals.
All inputs are finite; a program needn't handle non-finite values.
Results may differ from the reference program's by a relative error of at most 0.0003.
Values sent between devices are 32-bit elements; how exact they have to be, the bound alone decides.
No kernel may reach another device: no remote copies, remote signals or barrier semaphores. Data moves between devices by JAX's collectives and lax.ppermute only.
A program may use at most 128 MiB of HBM per device.

```python
import math
import jax
import jax.numpy as jnp
from jax import lax

D = 8192
TOK_DEV = 512
INNER_STEP = 100
ROWS = 512
TOKENS = 8192
REPLICAS = 16


def draw_drift(key, part):
    pieces = jax.random.split(key, 3)
    position = jnp.arange(ROWS, dtype=jnp.float32) / max(ROWS - 1, 1)
    row_scale = jnp.exp(position * math.log(3.0)) * jnp.exp(jax.random.uniform(pieces[1], (ROWS,), jnp.float32, 0.0, math.log(3.3)))
    col_scale = jnp.exp(jax.random.uniform(pieces[2], (D,), jnp.float32, 0.0, math.log(3.3)))
    base = jnp.clip(jax.random.normal(pieces[0], (REPLICAS, ROWS, D), jnp.float32), -6.0, 6.0)
    return (0.6 * base * row_scale[None, :, None] * col_scale[None, None, :]).astype(jnp.float32)


def spiked(values, stream_key, source, target, parts, factor):
    owner, partner = [(jnp.arange(values.shape[axis_at]) // (values.shape[axis_at] // parts)).reshape([-1 if axis == axis_at else 1 for axis in range(values.ndim)]) for axis_at in (source, target)]
    chosen = jax.random.permutation(stream_key, parts)[partner]
    strong = (owner == chosen) | (owner == (partner + parts // 2) % parts)
    return jnp.where(strong, factor * values, values)


def levels(own_key, shape, cuts, smallest, high):
    loudness = 1.0
    for axis_at, blocks in cuts:
        steps = jax.random.uniform(jax.random.fold_in(jax.random.fold_in(own_key, 6), axis_at), (blocks,), jnp.float32, smallest / len(cuts), high / len(cuts))
        loudness = loudness * jnp.repeat(jnp.exp(steps), shape[axis_at] // blocks).reshape((-1,) + (1,) * (len(shape) - 1 - axis_at))
    return loudness


def bell_draw(key, extent, scale, bound, cuts=(), kind=jnp.bfloat16):
    loudness = levels(key, extent, cuts, -0.22, 0.18) if cuts else 1.0
    drawn = jax.random.normal(key, extent, jnp.float32) * scale * loudness
    return jnp.minimum(jnp.maximum(drawn, -bound), bound).astype(kind)


def noise_with(key, dims, deviation, reach, cuts, heavy, kind=jnp.bfloat16):
    result = deviation * jax.random.normal(key, dims, jnp.float32)
    if cuts:
        result = result * levels(key, dims, cuts, -0.22, 0.18)
    return jnp.clip(spiked(result, jax.random.fold_in(key, 3), *heavy), -reach, reach).astype(kind)


def setup_inputs(seed: int = 0) -> dict:
    keys = jax.random.split(jax.random.key(seed), 8)
    return {
        "hidden_acts": noise_with(keys[0], (REPLICAS, TOKENS, ROWS), 1.0, 6.0, ((0, 16), (1, 16)), (1, 2, 16, 2.0)),
        "out_grads": bell_draw(keys[1], (REPLICAS, TOKENS, D), (TOKENS ** -0.5), 0.15625, ((0, 16), (1, 16))),
        "anchor": bell_draw(keys[2], (ROWS, D), 1.0, 6.0, ((0, 16),), jnp.float32),
        "drift": draw_drift(jax.random.fold_in(keys[7], 71), 0),
        "adam_first": bell_draw(keys[4], (REPLICAS, ROWS, D), 1.0, 6.0, ((0, 16), (1, 16)), jnp.float32),
        "adam_second": jnp.clip(jnp.exp(math.log(3.0) - 2.3025851 * jax.random.uniform(keys[5], (REPLICAS, ROWS, D), jnp.float32) ** levels(keys[5], (REPLICAS, ROWS, D), ((0, 16), (1, 16)), -0.2, 0.2)), 0.3, 3.0),
        "outer_momentum": bell_draw(keys[6], (ROWS, D), 0.5, 6.0, ((0, 16),), jnp.float32),
    }


beta_first = 0.9
beta_second = 0.95
inner_rate = 0.5
decay_weight = 0.1
outer_rate = 0.7
momentum_coef = 0.9

def replica_gradient(activations, cotangent):
    groups = TOKENS // TOK_DEV
    act_groups = activations.reshape(groups, TOK_DEV, ROWS)
    cot_groups = cotangent.reshape(groups, TOK_DEV, D)

    def accumulate(running, paired):
        partial_sum = jnp.dot(paired[0].T, paired[1], preferred_element_type=jnp.float32)
        return (running + partial_sum, None)
    summed, unused = lax.scan(accumulate, jnp.zeros((ROWS, D), jnp.float32), (act_groups, cot_groups))
    return summed

def reference(hidden_acts, out_grads, anchor, drift, adam_first, adam_second, outer_momentum):
    correction_one = 1.0 - beta_first ** INNER_STEP
    correction_two = 1.0 - beta_second ** INNER_STEP

    def per_replica(running, inputs):
        activations, cotangent, own_drift, first_old, second_old = inputs
        gradient = replica_gradient(activations, cotangent)
        moment_one = beta_first * first_old + (1.0 - beta_first) * gradient
        moment_two = beta_second * second_old + (1.0 - beta_second) * gradient * gradient
        update = moment_one / correction_one / (jnp.sqrt(moment_two / correction_two) + 1e-08) + decay_weight * (anchor + own_drift)
        pseudo = inner_rate * update - own_drift
        return (running + pseudo, (moment_one, moment_two))
    summed, moments = lax.scan(per_replica, jnp.zeros((ROWS, D), jnp.float32), (hidden_acts, out_grads, drift, adam_first, adam_second))
    new_first, new_second = moments
    average = summed / REPLICAS
    squares = jnp.sum(average * average)
    ceiling = 0.3 * math.sqrt(ROWS * D)
    factor = ceiling / jnp.maximum(jnp.sqrt(squares), ceiling)
    new_momentum = momentum_coef * outer_momentum + factor * average
    new_anchor = anchor - outer_rate * (factor * average + momentum_coef * new_momentum)
    return (new_first, new_second, new_momentum, new_anchor)
```

```python
import math

import jax
import jax.numpy as jnp
from jax import lax
from jax.sharding import Mesh, PartitionSpec as P

D = 8192
INNER_STEP = 100

beta_first = 0.9
beta_second = 0.95
inner_rate = 0.5
decay_weight = 0.1
outer_rate = 0.7
momentum_coef = 0.9

Y, X, Z, C = 4, 4, 8, 2
ROWS_DEV = 32
PARTS = Z * C
CHUNKS = 4
WIDTH = D // CHUNKS
HALF = WIDTH // 2
UP = [(i, (i + 1) % Z) for i in range(Z)]
DOWN = [(i, (i - 1) % Z) for i in range(Z)]
SWAP = [(0, 1), (1, 0)]


def reorder_rows(activations, z, c):
    rows = Z * C * ROWS_DEV
    place = lax.broadcasted_iota(jnp.int32, (rows, rows), 1)
    source = lax.broadcasted_iota(jnp.int32, (rows, rows), 0)
    mine = place // (Z * ROWS_DEV)
    core = jnp.where(mine == 1, c, 1 - c)
    step = (place // ROWS_DEV) % Z
    wanted = (((z + step) % Z) * C + core) * ROWS_DEV + place % ROWS_DEV
    pick = (wanted == source).astype(activations.dtype)
    return lax.dot_general(
        pick, activations, (((0,), (1,)), ((), ())), preferred_element_type=jnp.float32
    ).astype(activations.dtype)


def per_device(hidden_acts, out_grads, anchor, drift, adam_first, adam_second, outer_momentum):
    z = lax.axis_index("z")
    c = lax.axis_index("c")
    ordered = reorder_rows(hidden_acts[0], z, c)
    cotangent = out_grads[0]
    half_rows = Z * ROWS_DEV
    theirs, mine = ordered[:half_rows], ordered[half_rows:]

    def product(lhs, rhs):
        return lax.dot_general(lhs, rhs, (((1,), (0,)), ((), ())), preferred_element_type=jnp.float32)

    def ring(k, gate):
        cols = lax.slice_in_dim(cotangent, k * WIDTH, (k + 1) * WIDTH, axis=1)
        sent = product(theirs, cols)
        got = lax.ppermute(sent, "c", SWAP)
        kept = product(mine, cols)
        if gate is not None:
            got, _ = lax.optimization_barrier((got, gate))

        def own(j, lo=0, hi=WIDTH):
            j = j % Z
            r = slice(j * ROWS_DEV, (j + 1) * ROWS_DEV)
            return kept[r, lo:hi] + got[r, lo:hi]

        up = own(4, HALF, WIDTH)
        down = own(4, 0, HALF)
        for t in range(4):
            up = lax.ppermute(up, "z", UP)
            down = lax.ppermute(down, "z", DOWN)
            if t == 0:
                up = jnp.concatenate([own(3, 0, HALF), own(3, HALF, WIDTH) + up], axis=1)
                down = jnp.concatenate([own(5, 0, HALF) + down, own(5, HALF, WIDTH)], axis=1)
            elif t < 3:
                up = own(3 - t) + up
                down = own(5 + t) + down
            yield None
        yield own(0) + up + down

    done = [None] * CHUNKS
    for first in range(0, CHUNKS, 2):
        gate = None if first == 0 else done[first - 2][:8, :128]
        rings = [ring(k, gate) for k in (first, first + 1)]
        for t in range(5):
            for i in range(2):
                done[first + i] = next(rings[i])

    gradient = jnp.concatenate(done, axis=1)
    correction_one = 1.0 - beta_first**INNER_STEP
    correction_two = 1.0 - beta_second**INNER_STEP
    own_drift = drift[0]
    moment_one = beta_first * adam_first[0] + (1.0 - beta_first) * gradient
    moment_two = beta_second * adam_second[0] + (1.0 - beta_second) * gradient * gradient
    update = moment_one / correction_one / (
        jnp.sqrt(moment_two / correction_two) + 1e-08
    ) + decay_weight * (anchor + own_drift)
    pseudo = inner_rate * update - own_drift

    replicas = Y * X
    piece = D // replicas
    spread = pseudo.reshape(ROWS_DEV, replicas, piece).transpose(1, 0, 2)
    met = lax.all_to_all(spread, ("y", "x"), split_axis=0, concat_axis=0, tiled=True)
    part = jnp.sum(met, axis=0) / replicas
    copies = jnp.broadcast_to(part[None], (replicas, ROWS_DEV, piece))
    pieces = lax.all_to_all(copies, ("y", "x"), split_axis=0, concat_axis=0, tiled=True)
    average = pieces.transpose(1, 0, 2).reshape(ROWS_DEV, D)
    squares = jnp.broadcast_to(jnp.sum(pieces * pieces), (PARTS, 1, 128))
    squares = lax.all_to_all(squares, ("z", "c"), split_axis=0, concat_axis=0, tiled=True)
    squares = jnp.sum(squares[:, 0, 0])
    ceiling = 0.3 * math.sqrt(ROWS_DEV * PARTS * D)
    factor = ceiling / jnp.maximum(jnp.sqrt(squares), ceiling)
    momentum = momentum_coef * outer_momentum + factor * average
    updated = anchor - outer_rate * (factor * average + momentum_coef * momentum)
    return (moment_one[None], moment_two[None], momentum, updated)


def solution(mesh):
    devices = mesh.devices.reshape(Y, X, Z, C)
    grid = Mesh(devices, ("y", "x", "z", "c"))
    rep, fsdp = ("y", "x"), ("z", "c")
    return jax.shard_map(
        per_device,
        mesh=grid,
        in_specs=(
            P(rep, fsdp, None),
            P(rep, fsdp, None),
            P(fsdp, None),
            P(rep, fsdp, None),
            P(rep, fsdp, None),
            P(rep, fsdp, None),
            P(fsdp, None),
        ),
        out_specs=(
            P(rep, fsdp, None),
            P(rep, fsdp, None),
            P(fsdp, None),
            P(fsdp, None),
        ),
        check_vma=False,
    )
```

```python
import math

import jax
import jax.numpy as jnp
from jax import lax
from jax.sharding import Mesh, PartitionSpec as P

D = 8192
INNER_STEP = 100

beta_first = 0.9
beta_second = 0.95
inner_rate = 0.5
decay_weight = 0.1
outer_rate = 0.7
momentum_coef = 0.9

Y, X, Z, C = 4, 4, 8, 2
ROWS_DEV = 32
PARTS = Z * C
CHUNKS = 2
WIDTH = D // CHUNKS
HALF = WIDTH // 2
STEPS = (4, 3, 5, 2, 6, 1, 7, 0)
UP = [(i, (i + 1) % Z) for i in range(Z)]
DOWN = [(i, (i - 1) % Z) for i in range(Z)]
SWAP = [(0, 1), (1, 0)]


def reorder_rows(activations, z, c):
    rows = Z * C * ROWS_DEV
    place = lax.broadcasted_iota(jnp.int32, (rows, rows), 1)
    source = lax.broadcasted_iota(jnp.int32, (rows, rows), 0)
    mine = place // (Z * ROWS_DEV)
    core = jnp.where(mine == 1, c, 1 - c)
    slot = (place // ROWS_DEV) % Z
    step = jnp.zeros_like(slot)
    for at, distance in enumerate(STEPS):
        step = jnp.where(slot == at, distance, step)
    wanted = (((z + step) % Z) * C + core) * ROWS_DEV + place % ROWS_DEV
    pick = (wanted == source).astype(activations.dtype)
    return lax.dot_general(
        pick, activations, (((0,), (1,)), ((), ())), preferred_element_type=jnp.float32
    ).astype(activations.dtype)


def per_device(hidden_acts, out_grads, anchor, drift, adam_first, adam_second, outer_momentum):
    z = lax.axis_index("z")
    c = lax.axis_index("c")
    ordered = reorder_rows(hidden_acts[0], z, c)
    cotangent = out_grads[0]
    half_rows = Z * ROWS_DEV
    theirs, mine = ordered[:half_rows], ordered[half_rows:]

    def product(lhs, rhs):
        return lax.dot_general(lhs, rhs, (((1,), (0,)), ((), ())), preferred_element_type=jnp.float32)

    def after(values, *tokens):
        return lax.optimization_barrier((values, tokens))[0]

    chunks = range(CHUNKS)
    cols = [lax.slice_in_dim(cotangent, k * WIDTH, (k + 1) * WIDTH, axis=1) for k in chunks]
    first = [lax.ppermute(product(theirs[:ROWS_DEV], cols[k]), "c", SWAP) for k in chunks]
    kept = [None] * CHUNKS
    rest = [None] * CHUNKS
    up = [None] * CHUNKS
    down = [None] * CHUNKS

    def own(k, distance, lo=0, hi=WIDTH):
        at = STEPS.index(distance) * ROWS_DEV
        local = kept[k][at : at + ROWS_DEV, lo:hi]
        if at == 0:
            return local + first[k][:, lo:hi]
        return local + rest[k][at - ROWS_DEV : at, lo:hi]

    lhs = mine
    for k in chunks:
        kept[k] = product(lhs, cols[k])
        up[k] = own(k, 4, HALF, WIDTH)
        down[k] = own(k, 4, 0, HALF)
        lhs = after(mine, up[k], down[k])
    lhs = after(theirs[ROWS_DEV:], up[-1], down[-1])
    for k in chunks:
        sent = product(lhs, cols[k])
        rest[k] = lax.ppermute(sent, "c", SWAP)
        lhs = after(theirs[ROWS_DEV:], sent)
    last = (up[-1], down[-1])
    for t in range(1, 5):
        for k in chunks:
            moved = (lax.ppermute(up[k], "z", UP), lax.ppermute(down[k], "z", DOWN))
            u, d = after(moved, last)
            if t == 1:
                up[k] = jnp.concatenate([own(k, 3, 0, HALF), own(k, 3, HALF, WIDTH) + u], axis=1)
                down[k] = jnp.concatenate([own(k, 5, 0, HALF) + d, own(k, 5, HALF, WIDTH)], axis=1)
            elif t < 4:
                up[k] = own(k, 4 - t) + u
                down[k] = own(k, 4 + t) + d
            else:
                up[k] = down[k] = own(k, 0) + u + d
            last = (up[k], down[k])

    gradient = jnp.concatenate(up, axis=1)
    correction_one = 1.0 - beta_first**INNER_STEP
    correction_two = 1.0 - beta_second**INNER_STEP
    own_drift = drift[0]
    moment_one = beta_first * adam_first[0] + (1.0 - beta_first) * gradient
    moment_two = beta_second * adam_second[0] + (1.0 - beta_second) * gradient * gradient
    update = moment_one / correction_one / (
        jnp.sqrt(moment_two / correction_two) + 1e-08
    ) + decay_weight * (anchor + own_drift)
    pseudo = inner_rate * update - own_drift

    replicas = Y * X
    piece = D // replicas
    spread = pseudo.reshape(ROWS_DEV, replicas, piece).transpose(1, 0, 2)
    met = lax.all_to_all(spread, ("y", "x"), split_axis=0, concat_axis=0, tiled=True)
    part = jnp.sum(met, axis=0) / replicas
    copies = jnp.broadcast_to(part[None], (replicas, ROWS_DEV, piece))
    pieces = lax.all_to_all(copies, ("y", "x"), split_axis=0, concat_axis=0, tiled=True)
    average = pieces.transpose(1, 0, 2).reshape(ROWS_DEV, D)
    squares = jnp.broadcast_to(jnp.sum(pieces * pieces), (PARTS, 1, 128))
    squares = lax.all_to_all(squares, ("z", "c"), split_axis=0, concat_axis=0, tiled=True)
    squares = jnp.sum(squares[:, 0, 0])
    ceiling = 0.3 * math.sqrt(ROWS_DEV * PARTS * D)
    factor = ceiling / jnp.maximum(jnp.sqrt(squares), ceiling)
    momentum = momentum_coef * outer_momentum + factor * average
    updated = anchor - outer_rate * (factor * average + momentum_coef * momentum)
    return (moment_one[None], moment_two[None], momentum, updated)


def solution(mesh):
    devices = mesh.devices.reshape(Y, X, Z, C)
    grid = Mesh(devices, ("y", "x", "z", "c"))
    rep, fsdp = ("y", "x"), ("z", "c")
    return jax.shard_map(
        per_device,
        mesh=grid,
        in_specs=(
            P(rep, fsdp, None),
            P(rep, fsdp, None),
            P(fsdp, None),
            P(rep, fsdp, None),
            P(rep, fsdp, None),
            P(rep, fsdp, None),
            P(fsdp, None),
        ),
        out_specs=(
            P(rep, fsdp, None),
            P(rep, fsdp, None),
            P(fsdp, None),
            P(fsdp, None),
        ),
        check_vma=False,
    )
```

```python
import math

import jax
import jax.numpy as jnp
from jax import lax
from jax.experimental import pallas as pl
from jax.experimental.pallas import tpu as pltpu
from jax.sharding import Mesh, PartitionSpec as P

D = 8192
INNER_STEP = 100

beta_first = 0.9
beta_second = 0.95
inner_rate = 0.5
decay_weight = 0.1
outer_rate = 0.7
momentum_coef = 0.9

Y, X, Z, C = 4, 4, 8, 2
ROWS_DEV = 32
PARTS = Z * C
CHUNKS = 2
WIDTH = D // CHUNKS
HALF = WIDTH // 2
STEPS = (4, 3, 5, 2, 6, 1, 7, 0)
UP = [(i, (i + 1) % Z) for i in range(Z)]
DOWN = [(i, (i - 1) % Z) for i in range(Z)]
SWAP = [(0, 1), (1, 0)]


def reorder_rows(activations, z, c):
    rows = Z * C * ROWS_DEV
    place = lax.broadcasted_iota(jnp.int32, (rows, rows), 1)
    source = lax.broadcasted_iota(jnp.int32, (rows, rows), 0)
    mine = place // (Z * ROWS_DEV)
    core = jnp.where(mine == 1, c, 1 - c)
    slot = (place // ROWS_DEV) % Z
    step = jnp.zeros_like(slot)
    for at, distance in enumerate(STEPS):
        step = jnp.where(slot == at, distance, step)
    wanted = (((z + step) % Z) * C + core) * ROWS_DEV + place % ROWS_DEV
    pick = (wanted == source).astype(activations.dtype)
    return lax.dot_general(
        pick, activations, (((0,), (1,)), ((), ())), preferred_element_type=jnp.float32
    ).astype(activations.dtype)


def square_kernel(pieces_ref, out_ref):
    def add(p, total):
        x = pieces_ref[p]
        x = x * x
        for r in range(0, ROWS_DEV, 8):
            for l in range(0, x.shape[1], 128):
                total = total + x[r : r + 8, l : l + 128]
        return total

    total = lax.fori_loop(0, pieces_ref.shape[0], add, jnp.zeros((8, 128), jnp.float32))
    out_ref[...] = jnp.broadcast_to(total[None], out_ref.shape)


def squares_of(pieces):
    return pl.pallas_call(
        square_kernel,
        out_shape=jax.ShapeDtypeStruct((PARTS, 8, 128), jnp.float32),
        cost_estimate=pl.CostEstimate(flops=2 * pieces.size, bytes_accessed=4 * pieces.size, transcendentals=0),
    )(pieces)


def finish_kernel(squares_ref, pieces_ref, anchor_ref, momentum_ref, momentum_out, anchor_out):
    squares = jnp.sum(jnp.sum(squares_ref[...], axis=0), keepdims=True)
    ceiling = 0.3 * math.sqrt(ROWS_DEV * PARTS * D)
    factor = ceiling / jnp.maximum(jnp.sqrt(squares), ceiling)
    piece = pieces_ref.shape[2]
    for p in range(pieces_ref.shape[0]):
        at = slice(p * piece, (p + 1) * piece)
        scaled = factor * pieces_ref[p]
        momentum = momentum_coef * momentum_ref[:, at] + scaled
        momentum_out[:, at] = momentum
        anchor_out[:, at] = anchor_ref[:, at] - outer_rate * (scaled + momentum_coef * momentum)


def finish(squares, pieces, anchor, outer_momentum):
    replicas, _, both = pieces.shape
    part = pl.BlockSpec((ROWS_DEV, WIDTH), lambda h: (0, h))
    shape = jax.ShapeDtypeStruct(anchor.shape, jnp.float32)
    return pl.pallas_call(
        finish_kernel,
        grid=(CHUNKS,),
        in_specs=[
            pl.BlockSpec(squares.shape, lambda h: (0, 0, 0)),
            pl.BlockSpec((replicas, ROWS_DEV, both // CHUNKS), lambda h: (0, 0, h)),
            part,
            part,
        ],
        out_specs=[part, part],
        out_shape=[shape, shape],
        cost_estimate=pl.CostEstimate(flops=7 * anchor.size, bytes_accessed=20 * anchor.size, transcendentals=0),
    )(squares, pieces, anchor, outer_momentum)


def per_device(hidden_acts, out_grads, anchor, drift, adam_first, adam_second, outer_momentum):
    z = lax.axis_index("z")
    c = lax.axis_index("c")
    ordered = reorder_rows(hidden_acts[0], z, c)
    cotangent = out_grads[0]
    half_rows = Z * ROWS_DEV
    theirs, mine = ordered[:half_rows], ordered[half_rows:]

    def product(lhs, rhs):
        return lax.dot_general(lhs, rhs, (((1,), (0,)), ((), ())), preferred_element_type=jnp.float32)

    def after(values, *tokens):
        return lax.optimization_barrier((values, tokens))[0]

    chunks = range(CHUNKS)
    cols = [lax.slice_in_dim(cotangent, k * WIDTH, (k + 1) * WIDTH, axis=1) for k in chunks]
    first = [lax.ppermute(product(theirs[:ROWS_DEV], cols[k]), "c", SWAP) for k in chunks]
    kept = [None] * CHUNKS
    rest = [None] * CHUNKS
    up = [None] * CHUNKS
    down = [None] * CHUNKS

    def own(k, distance, lo=0, hi=WIDTH):
        at = STEPS.index(distance) * ROWS_DEV
        local = kept[k][at : at + ROWS_DEV, lo:hi]
        if at == 0:
            return local + first[k][:, lo:hi]
        return local + rest[k][at - ROWS_DEV : at, lo:hi]

    def start_ring(k, lhs):
        kept[k] = product(lhs, cols[k])
        up[k] = own(k, 4, HALF, WIDTH)
        down[k] = own(k, 4, 0, HALF)

    def swap_rest(k, lhs):
        sent = product(lhs, cols[k])
        rest[k] = lax.ppermute(sent, "c", SWAP)
        return sent

    def move(k, *tokens):
        moved = (lax.ppermute(up[k], "z", UP), lax.ppermute(down[k], "z", DOWN))
        return after(moved, *tokens)

    def step(k, t, u, d):
        if t == 1:
            up[k] = jnp.concatenate([own(k, 3, 0, HALF), own(k, 3, HALF, WIDTH) + u], axis=1)
            down[k] = jnp.concatenate([own(k, 5, 0, HALF) + d, own(k, 5, HALF, WIDTH)], axis=1)
        else:
            up[k] = own(k, 4 - t) + u
            down[k] = own(k, 4 + t) + d

    correction_one = 1.0 - beta_first**INNER_STEP
    correction_two = 1.0 - beta_second**INNER_STEP
    replicas = Y * X
    piece = WIDTH // replicas

    def moments(first_old, second_old, gradient):
        moment_one = beta_first * first_old + (1.0 - beta_first) * gradient
        moment_two = beta_second * second_old + (1.0 - beta_second) * gradient * gradient
        return moment_one, moment_two

    def meet(k, gradient):
        at = slice(k * WIDTH, (k + 1) * WIDTH)
        own_drift = drift[0, :, at]
        moment_one, moment_two = moments(adam_first[0, :, at], adam_second[0, :, at], gradient)
        update = moment_one / correction_one / (
            jnp.sqrt(moment_two / correction_two) + 1e-08
        ) + decay_weight * (anchor[:, at] + own_drift)
        pseudo = inner_rate * update - own_drift
        spread = pseudo.reshape(ROWS_DEV, replicas, piece).transpose(1, 0, 2)
        return lax.all_to_all(spread, ("y", "x"), split_axis=0, concat_axis=0, tiled=True)

    start_ring(0, mine)
    sent = swap_rest(0, after(theirs[ROWS_DEV:], up[0], down[0]))
    start_ring(1, after(mine, sent))
    step(0, 1, *move(0, up[1], down[1]))
    u, d = move(1, up[0], down[0])
    swap_rest(1, after(theirs[ROWS_DEV:], up[0], down[0]))
    step(1, 1, u, d)
    for t in (2, 3):
        step(0, t, *move(0, up[1], down[1]))
        step(1, t, *move(1, up[0], down[0]))
    u, d = move(0, up[1], down[1])
    gradients = [own(0, 0) + u + d]
    met = [meet(0, gradients[0])]
    u, d = move(1, met[0])
    gradients.append(own(1, 0) + u + d)
    met.append(meet(1, gradients[1]))

    gradient = jnp.concatenate(gradients, axis=1)
    moment_one, moment_two = moments(adam_first[0], adam_second[0], gradient)
    part = jnp.concatenate([jnp.sum(m, axis=0) / replicas for m in met], axis=1)
    copies = jnp.broadcast_to(part[None], (replicas, ROWS_DEV, CHUNKS * piece))
    pieces = lax.all_to_all(copies, ("y", "x"), split_axis=0, concat_axis=0, tiled=True)
    squares = lax.all_to_all(squares_of(pieces), ("z", "c"), split_axis=0, concat_axis=0, tiled=True)
    momentum, updated = finish(squares, pieces, anchor, outer_momentum)
    return (moment_one[None], moment_two[None], momentum, updated)


def solution(mesh):
    devices = mesh.devices.reshape(Y, X, Z, C)
    grid = Mesh(devices, ("y", "x", "z", "c"))
    rep, fsdp = ("y", "x"), ("z", "c")
    return jax.shard_map(
        per_device,
        mesh=grid,
        in_specs=(
            P(rep, fsdp, None),
            P(rep, fsdp, None),
            P(fsdp, None),
            P(rep, fsdp, None),
            P(rep, fsdp, None),
            P(rep, fsdp, None),
            P(fsdp, None),
        ),
        out_specs=(
            P(rep, fsdp, None),
            P(rep, fsdp, None),
            P(fsdp, None),
            P(fsdp, None),
        ),
        check_vma=False,
    )
```

```python
import math

import jax
import jax.numpy as jnp
from jax import lax
from jax.experimental import pallas as pl
from jax.experimental.pallas import tpu as pltpu
from jax.sharding import Mesh, PartitionSpec as P

D = 8192
INNER_STEP = 100

beta_first = 0.9
beta_second = 0.95
inner_rate = 0.5
decay_weight = 0.1
outer_rate = 0.7
momentum_coef = 0.9

Y, X, Z, C = 4, 4, 8, 2
ROWS_DEV = 32
PARTS = Z * C
CHUNKS = 2
WIDTH = D // CHUNKS
HALF = WIDTH // 2
STEPS = (4, 3, 5, 2, 6, 1, 7, 0)
UP = [(i, (i + 1) % Z) for i in range(Z)]
DOWN = [(i, (i - 1) % Z) for i in range(Z)]
SWAP = [(0, 1), (1, 0)]


def reorder_rows(activations, z, c):
    rows = Z * C * ROWS_DEV
    place = lax.broadcasted_iota(jnp.int32, (rows, rows), 1)
    source = lax.broadcasted_iota(jnp.int32, (rows, rows), 0)
    block = place // ROWS_DEV
    mine = jnp.where(block < 2, block == 1, block >= 2 + (Z - 1))
    slot = jnp.where(block < 2, 0, jnp.where(block < Z + 1, block - 1, block - Z))
    step = jnp.zeros_like(slot)
    for at, distance in enumerate(STEPS):
        step = jnp.where(slot == at, distance, step)
    core = jnp.where(mine, c, 1 - c)
    wanted = (((z + step) % Z) * C + core) * ROWS_DEV + place % ROWS_DEV
    pick = (wanted == source).astype(activations.dtype)
    return lax.dot_general(
        pick, activations, (((0,), (1,)), ((), ())), preferred_element_type=jnp.float32
    ).astype(activations.dtype)


def head_kernel(rows_ref, cols_ref, theirs_ref, mine_ref):
    out = jnp.dot(rows_ref[...], cols_ref[...], preferred_element_type=jnp.float32)
    theirs_ref[...] = out[:ROWS_DEV]
    mine_ref[...] = out[ROWS_DEV:]


def head_rows(ordered, cotangent, k):
    tokens = cotangent.shape[0]
    block = 1024
    count = WIDTH // block
    out = pl.BlockSpec((ROWS_DEV, block), lambda n: (0, n))
    shape = jax.ShapeDtypeStruct((ROWS_DEV, WIDTH), jnp.float32)
    return pl.pallas_call(
        head_kernel,
        grid=(count,),
        in_specs=[
            pl.BlockSpec((2 * ROWS_DEV, tokens), lambda n: (0, 0)),
            pl.BlockSpec((tokens, block), lambda n: (0, k * count + n)),
        ],
        out_specs=[out, out],
        out_shape=[shape, shape],
        cost_estimate=pl.CostEstimate(
            flops=4 * ROWS_DEV * tokens * WIDTH,
            bytes_accessed=2 * tokens * WIDTH + 8 * ROWS_DEV * WIDTH,
            transcendentals=0,
        ),
    )(ordered, cotangent)


def finish_kernel(squares_ref, pieces_ref, anchor_ref, momentum_ref, momentum_out, anchor_out):
    squares = jnp.sum(squares_ref[:, 0, 0:1], axis=0, keepdims=True)
    ceiling = 0.3 * math.sqrt(ROWS_DEV * PARTS * D)
    factor = ceiling / jnp.maximum(jnp.sqrt(squares), ceiling)
    piece = pieces_ref.shape[2]
    for p in range(pieces_ref.shape[0]):
        at = slice(p * piece, (p + 1) * piece)
        scaled = factor * pieces_ref[p]
        momentum = momentum_coef * momentum_ref[:, at] + scaled
        momentum_out[:, at] = momentum
        anchor_out[:, at] = anchor_ref[:, at] - outer_rate * (scaled + momentum_coef * momentum)


def finish(squares, pieces, anchor, outer_momentum):
    replicas, _, piece = pieces.shape
    parts = 2
    part = pl.BlockSpec((ROWS_DEV, D // parts), lambda h: (0, h))
    shape = jax.ShapeDtypeStruct(anchor.shape, jnp.float32)
    return pl.pallas_call(
        finish_kernel,
        grid=(parts,),
        in_specs=[
            pl.BlockSpec(squares.shape, lambda h: (0, 0, 0)),
            pl.BlockSpec((replicas // parts, ROWS_DEV, piece), lambda h: (h, 0, 0)),
            part,
            part,
        ],
        out_specs=[part, part],
        out_shape=[shape, shape],
        cost_estimate=pl.CostEstimate(flops=7 * anchor.size, bytes_accessed=20 * anchor.size, transcendentals=0),
    )(squares, pieces, anchor, outer_momentum)


def per_device(hidden_acts, out_grads, anchor, drift, adam_first, adam_second, outer_momentum):
    z = lax.axis_index("z")
    c = lax.axis_index("c")
    ordered = reorder_rows(hidden_acts[0], z, c)
    cotangent = out_grads[0]
    near = 2 * ROWS_DEV
    stay = near + (Z - 1) * ROWS_DEV

    def product(lhs, rhs):
        return lax.dot_general(lhs, rhs, (((1,), (0,)), ((), ())), preferred_element_type=jnp.float32)

    def after(values, *tokens):
        return lax.optimization_barrier((values, tokens))[0]

    chunks = range(CHUNKS)
    cols = [lax.slice_in_dim(cotangent, k * WIDTH, (k + 1) * WIDTH, axis=1) for k in chunks]
    up = [None] * CHUNKS
    down = [None] * CHUNKS

    def own(k, distance, lo=0, hi=WIDTH):
        at = (STEPS.index(distance) - 1) * ROWS_DEV
        base = k * WIDTH
        return kept[k][at : at + ROWS_DEV, lo:hi] + rest[at : at + ROWS_DEV, base + lo : base + hi]

    first_rows = ordered[:near]
    last = ()
    for k in chunks:
        sent, stays = head_rows(first_rows, cotangent, k)
        first = stays + after(lax.ppermute(sent, "c", SWAP), last)
        up[k], down[k] = first[:, HALF:], first[:, :HALF]
        first_rows = after(first_rows, sent)
        last = (up[k], down[k])
    last = (up[-1], down[-1])
    sent = product(after(ordered[near:stay], last), cotangent)
    rest = lax.ppermute(sent, "c", SWAP)
    lhs = after(ordered[stay:], sent)
    kept = [product(lhs, cols[k]) for k in chunks]
    for t in range(1, 5):
        for k in chunks:
            moved = (lax.ppermute(up[k], "z", UP), lax.ppermute(down[k], "z", DOWN))
            u, d = after(moved, last)
            if t == 1:
                up[k] = jnp.concatenate([own(k, 3, 0, HALF), own(k, 3, HALF, WIDTH) + u], axis=1)
                down[k] = jnp.concatenate([own(k, 5, 0, HALF) + d, own(k, 5, HALF, WIDTH)], axis=1)
            elif t < 4:
                up[k] = own(k, 4 - t) + u
                down[k] = own(k, 4 + t) + d
            else:
                up[k] = down[k] = own(k, 0) + u + d
            last = (up[k], down[k])

    gradient = jnp.concatenate(up, axis=1)
    correction_one = 1.0 - beta_first**INNER_STEP
    correction_two = 1.0 - beta_second**INNER_STEP
    own_drift = drift[0]
    moment_one = beta_first * adam_first[0] + (1.0 - beta_first) * gradient
    moment_two = beta_second * adam_second[0] + (1.0 - beta_second) * gradient * gradient
    update = moment_one / correction_one / (
        jnp.sqrt(moment_two / correction_two) + 1e-08
    ) + decay_weight * (anchor + own_drift)
    pseudo = inner_rate * update - own_drift

    replicas = Y * X
    piece = D // replicas
    spread = pseudo.reshape(ROWS_DEV, replicas, piece).transpose(1, 0, 2)
    met = lax.all_to_all(spread, ("y", "x"), split_axis=0, concat_axis=0, tiled=True)
    part = jnp.sum(met, axis=0) / replicas
    copies = jnp.broadcast_to(part[None], (replicas, ROWS_DEV, piece))
    pieces = lax.all_to_all(copies, ("y", "x"), split_axis=0, concat_axis=0, tiled=True)
    squares = jnp.broadcast_to(jnp.sum(pieces * pieces), (PARTS, 1, 128))
    squares = lax.all_to_all(squares, ("z", "c"), split_axis=0, concat_axis=0, tiled=True)
    momentum, updated = finish(squares, pieces, anchor, outer_momentum)
    return (moment_one[None], moment_two[None], momentum, updated)


def solution(mesh):
    devices = mesh.devices.reshape(Y, X, Z, C)
    grid = Mesh(devices, ("y", "x", "z", "c"))
    rep, fsdp = ("y", "x"), ("z", "c")
    return jax.shard_map(
        per_device,
        mesh=grid,
        in_specs=(
            P(rep, fsdp, None),
            P(rep, fsdp, None),
            P(fsdp, None),
            P(rep, fsdp, None),
            P(rep, fsdp, None),
            P(rep, fsdp, None),
            P(fsdp, None),
        ),
        out_specs=(
            P(rep, fsdp, None),
            P(rep, fsdp, None),
            P(fsdp, None),
            P(fsdp, None),
        ),
        check_vma=False,
    )
```

```python
import math

import jax
import jax.numpy as jnp
from jax import lax
from jax.experimental import pallas as pl
from jax.experimental.pallas import tpu as pltpu
from jax.sharding import Mesh, PartitionSpec as P

D = 8192
INNER_STEP = 100

beta_first = 0.9
beta_second = 0.95
inner_rate = 0.5
decay_weight = 0.1
outer_rate = 0.7
momentum_coef = 0.9

Y, X, Z, C = 4, 4, 8, 2
ROWS_DEV = 32
PARTS = Z * C
CHUNKS = 2
WIDTH = D // CHUNKS
HALF = WIDTH // 2
STEPS = (4, 3, 5, 2, 6, 1, 7, 0)
UP = [(i, (i + 1) % Z) for i in range(Z)]
DOWN = [(i, (i - 1) % Z) for i in range(Z)]
SWAP = [(0, 1), (1, 0)]


def reorder_rows(activations, z, c):
    rows = Z * C * ROWS_DEV
    place = lax.broadcasted_iota(jnp.int32, (rows, rows), 1)
    source = lax.broadcasted_iota(jnp.int32, (rows, rows), 0)
    block = place // ROWS_DEV
    mine = jnp.where(block < 2, block == 1, block >= 2 + (Z - 1))
    slot = jnp.where(block < 2, 0, jnp.where(block < Z + 1, block - 1, block - Z))
    step = jnp.zeros_like(slot)
    for at, distance in enumerate(STEPS):
        step = jnp.where(slot == at, distance, step)
    core = jnp.where(mine, c, 1 - c)
    wanted = (((z + step) % Z) * C + core) * ROWS_DEV + place % ROWS_DEV
    pick = (wanted == source).astype(activations.dtype)
    return lax.dot_general(
        pick, activations, (((0,), (1,)), ((), ())), preferred_element_type=jnp.float32
    ).astype(activations.dtype)


def finish_kernel(squares_ref, pieces_ref, anchor_ref, momentum_ref, momentum_out, anchor_out):
    squares = jnp.sum(jnp.sum(squares_ref[...], axis=0), keepdims=True)
    ceiling = 0.3 * math.sqrt(ROWS_DEV * PARTS * D)
    factor = ceiling / jnp.maximum(jnp.sqrt(squares), ceiling)
    piece = pieces_ref.shape[2]
    for p in range(pieces_ref.shape[0]):
        at = slice(p * piece, (p + 1) * piece)
        scaled = factor * pieces_ref[p]
        momentum = momentum_coef * momentum_ref[:, at] + scaled
        momentum_out[:, at] = momentum
        anchor_out[:, at] = anchor_ref[:, at] - outer_rate * (scaled + momentum_coef * momentum)


def finish(squares, pieces, anchor, outer_momentum):
    replicas, _, piece = pieces.shape
    parts = 2
    part = pl.BlockSpec((ROWS_DEV, D // parts), lambda h: (0, h))
    shape = jax.ShapeDtypeStruct(anchor.shape, jnp.float32)
    return pl.pallas_call(
        finish_kernel,
        grid=(parts,),
        in_specs=[
            pl.BlockSpec(squares.shape, lambda h: (0, 0, 0)),
            pl.BlockSpec((replicas // parts, ROWS_DEV, piece), lambda h: (h, 0, 0)),
            part,
            part,
        ],
        out_specs=[part, part],
        out_shape=[shape, shape],
        cost_estimate=pl.CostEstimate(flops=7 * anchor.size, bytes_accessed=20 * anchor.size, transcendentals=0),
    )(squares, pieces, anchor, outer_momentum)


def per_device(hidden_acts, out_grads, anchor, drift, adam_first, adam_second, outer_momentum):
    z = lax.axis_index("z")
    c = lax.axis_index("c")
    ordered = reorder_rows(hidden_acts[0], z, c)
    cotangent = out_grads[0]
    near = 2 * ROWS_DEV
    stay = near + (Z - 1) * ROWS_DEV

    def product(lhs, rhs):
        return lax.dot_general(lhs, rhs, (((1,), (0,)), ((), ())), preferred_element_type=jnp.float32)

    def after(values, *tokens):
        return lax.optimization_barrier((values, tokens))[0]

    chunks = range(CHUNKS)
    cols = [lax.slice_in_dim(cotangent, k * WIDTH, (k + 1) * WIDTH, axis=1) for k in chunks]
    up = [None] * CHUNKS
    down = [None] * CHUNKS

    def own(k, distance, lo=0, hi=WIDTH):
        at = (STEPS.index(distance) - 1) * ROWS_DEV
        base = k * WIDTH
        return kept[k][at : at + ROWS_DEV, lo:hi] + rest[at : at + ROWS_DEV, base + lo : base + hi]

    first = product(ordered[:near], cotangent)
    theirs = lax.optimization_barrier(first[:ROWS_DEV])
    got = lax.ppermute(theirs, "c", SWAP)
    sent = product(after(ordered[near:stay], theirs), cotangent)
    rest = lax.ppermute(after(sent, got), "c", SWAP)
    first = first[ROWS_DEV:] + got
    for k in chunks:
        up[k] = first[:, k * WIDTH + HALF : (k + 1) * WIDTH]
        down[k] = first[:, k * WIDTH : k * WIDTH + HALF]
        first = after(first, up[k], down[k])
    last = (up[-1], down[-1])
    lhs = after(ordered[stay:], sent, last)
    kept = [product(lhs, cols[k]) for k in chunks]
    for t in range(1, 5):
        for k in chunks:
            moved = (lax.ppermute(up[k], "z", UP), lax.ppermute(down[k], "z", DOWN))
            u, d = after(moved, last)
            if t == 1:
                up[k] = jnp.concatenate([own(k, 3, 0, HALF), own(k, 3, HALF, WIDTH) + u], axis=1)
                down[k] = jnp.concatenate([own(k, 5, 0, HALF) + d, own(k, 5, HALF, WIDTH)], axis=1)
            elif t < 4:
                up[k] = own(k, 4 - t) + u
                down[k] = own(k, 4 + t) + d
            else:
                up[k] = down[k] = own(k, 0) + u + d
            last = (up[k], down[k])

    gradient = jnp.concatenate(up, axis=1)
    correction_one = 1.0 - beta_first**INNER_STEP
    correction_two = 1.0 - beta_second**INNER_STEP
    own_drift = drift[0]
    moment_one = beta_first * adam_first[0] + (1.0 - beta_first) * gradient
    moment_two = beta_second * adam_second[0] + (1.0 - beta_second) * gradient * gradient
    update = moment_one / correction_one / (
        jnp.sqrt(moment_two / correction_two) + 1e-08
    ) + decay_weight * (anchor + own_drift)
    pseudo = inner_rate * update - own_drift

    replicas = Y * X
    piece = D // replicas
    spread = pseudo.reshape(ROWS_DEV, replicas, piece).transpose(1, 0, 2)
    met = lax.all_to_all(spread, ("y", "x"), split_axis=0, concat_axis=0, tiled=True)
    part = jnp.sum(met, axis=0) / replicas
    copies = jnp.broadcast_to(part[None], (replicas, ROWS_DEV, piece))
    pieces = lax.all_to_all(copies, ("y", "x"), split_axis=0, concat_axis=0, tiled=True)
    squares = jnp.sum(jnp.sum(pieces * pieces, axis=(0, 1)).reshape(-1, 128), axis=0)
    squares = jnp.broadcast_to(squares, (PARTS, 1, 128))
    squares = lax.all_to_all(squares, ("z", "c"), split_axis=0, concat_axis=0, tiled=True)
    momentum, updated = finish(squares, pieces, anchor, outer_momentum)
    return (moment_one[None], moment_two[None], momentum, updated)


def solution(mesh):
    devices = mesh.devices.reshape(Y, X, Z, C)
    grid = Mesh(devices, ("y", "x", "z", "c"))
    rep, fsdp = ("y", "x"), ("z", "c")
    return jax.shard_map(
        per_device,
        mesh=grid,
        in_specs=(
            P(rep, fsdp, None),
            P(rep, fsdp, None),
            P(fsdp, None),
            P(rep, fsdp, None),
            P(rep, fsdp, None),
            P(rep, fsdp, None),
            P(fsdp, None),
        ),
        out_specs=(
            P(rep, fsdp, None),
            P(rep, fsdp, None),
            P(fsdp, None),
            P(fsdp, None),
        ),
        check_vma=False,
    )
```

```python
import math

import jax
import jax.numpy as jnp
from jax import lax
from jax.experimental import pallas as pl
from jax.experimental.pallas import tpu as pltpu
from jax.sharding import Mesh, PartitionSpec as P

D = 8192
INNER_STEP = 100

beta_first = 0.9
beta_second = 0.95
inner_rate = 0.5
decay_weight = 0.1
outer_rate = 0.7
momentum_coef = 0.9

Y, X, Z, C = 4, 4, 8, 2
ROWS_DEV = 32
PARTS = Z * C
CHUNKS = ((0, D // 2), (D // 2, D // 2))
SHARES = ((0, D // 4), (D // 4, 3 * D // 4))
STEPS = (4, 3, 5, 2, 6, 1, 7, 0)
UP = [(i, (i + 1) % Z) for i in range(Z)]
DOWN = [(i, (i - 1) % Z) for i in range(Z)]
SWAP = [(0, 1), (1, 0)]


def reorder_rows(activations, z, c):
    rows = Z * C * ROWS_DEV
    place = lax.broadcasted_iota(jnp.int32, (rows, rows), 1)
    source = lax.broadcasted_iota(jnp.int32, (rows, rows), 0)
    block = place // ROWS_DEV
    mine = jnp.where(block < 2, block == 1, block >= 2 + (Z - 1))
    slot = jnp.where(block < 2, 0, jnp.where(block < Z + 1, block - 1, block - Z))
    step = jnp.zeros_like(slot)
    for at, distance in enumerate(STEPS):
        step = jnp.where(slot == at, distance, step)
    core = jnp.where(mine, c, 1 - c)
    wanted = (((z + step) % Z) * C + core) * ROWS_DEV + place % ROWS_DEV
    pick = (wanted == source).astype(activations.dtype)
    return lax.dot_general(
        pick, activations, (((0,), (1,)), ((), ())), preferred_element_type=jnp.float32
    ).astype(activations.dtype)


def finish_kernel(squares_ref, pieces_ref, anchor_ref, momentum_ref, momentum_out, anchor_out):
    squares = jnp.sum(jnp.sum(squares_ref[...], axis=0), keepdims=True)
    ceiling = 0.3 * math.sqrt(ROWS_DEV * PARTS * D)
    factor = ceiling / jnp.maximum(jnp.sqrt(squares), ceiling)
    replicas = pieces_ref.shape[0]
    for p in range(replicas):
        lane = 0
        for lo, width in SHARES:
            piece = width // replicas
            at = slice(lo + p * piece, lo + (p + 1) * piece)
            scaled = factor * pieces_ref[p, :, lane : lane + piece]
            momentum = momentum_coef * momentum_ref[:, at] + scaled
            momentum_out[:, at] = momentum
            anchor_out[:, at] = anchor_ref[:, at] - outer_rate * (scaled + momentum_coef * momentum)
            lane += piece


def finish(squares, pieces, anchor, outer_momentum):
    replicas, rows, share = pieces.shape
    block = 8
    part = pl.BlockSpec((block, D), lambda r: (r, 0))
    shape = jax.ShapeDtypeStruct(anchor.shape, jnp.float32)
    return pl.pallas_call(
        finish_kernel,
        grid=(rows // block,),
        in_specs=[
            pl.BlockSpec(squares.shape, lambda r: (0, 0, 0)),
            pl.BlockSpec((replicas, block, share), lambda r: (0, r, 0)),
            part,
            part,
        ],
        out_specs=[part, part],
        out_shape=[shape, shape],
        cost_estimate=pl.CostEstimate(flops=7 * anchor.size, bytes_accessed=20 * anchor.size, transcendentals=0),
    )(squares, pieces, anchor, outer_momentum)


def per_device(hidden_acts, out_grads, anchor, drift, adam_first, adam_second, outer_momentum):
    z = lax.axis_index("z")
    c = lax.axis_index("c")
    ordered = reorder_rows(hidden_acts[0], z, c)
    cotangent = out_grads[0]
    near = 2 * ROWS_DEV
    stay = near + (Z - 1) * ROWS_DEV

    def product(lhs, rhs):
        return lax.dot_general(lhs, rhs, (((1,), (0,)), ((), ())), preferred_element_type=jnp.float32)

    def after(values, *tokens):
        return lax.optimization_barrier((values, tokens))[0]

    chunks = range(len(CHUNKS))
    up = [None] * len(CHUNKS)
    down = [None] * len(CHUNKS)

    def own(k, distance, lo=0, hi=None):
        at = (STEPS.index(distance) - 1) * ROWS_DEV
        base, width = CHUNKS[k]
        hi = width if hi is None else hi
        return kept[k][at : at + ROWS_DEV, lo:hi] + rest[at : at + ROWS_DEV, base + lo : base + hi]

    first = product(ordered[:near], cotangent)
    theirs = lax.optimization_barrier(first[:ROWS_DEV])
    got = lax.ppermute(theirs, "c", SWAP)
    sent = product(after(ordered[near:stay], theirs), cotangent)
    rest = lax.ppermute(after(sent, got), "c", SWAP)
    first = first[ROWS_DEV:] + got
    for k, (lo, width) in enumerate(CHUNKS):
        up[k] = first[:, lo + width // 2 : lo + width]
        down[k] = first[:, lo : lo + width // 2]
        first = after(first, up[k], down[k])
    last = (up[-1], down[-1])
    lhs = after(ordered[stay:], sent, last)
    kept = [product(lhs, cotangent[:, lo : lo + width]) for lo, width in CHUNKS]
    for t in range(1, 4):
        for k in chunks:
            moved = (lax.ppermute(up[k], "z", UP), lax.ppermute(down[k], "z", DOWN))
            u, d = after(moved, last)
            if t == 1:
                half = CHUNKS[k][1] // 2
                up[k] = jnp.concatenate([own(k, 3, 0, half), own(k, 3, half) + u], axis=1)
                down[k] = jnp.concatenate([own(k, 5, 0, half) + d, own(k, 5, half)], axis=1)
            else:
                up[k] = own(k, 4 - t) + u
                down[k] = own(k, 4 + t) + d
            last = (up[k], down[k])

    correction_one = 1.0 - beta_first**INNER_STEP
    correction_two = 1.0 - beta_second**INNER_STEP
    replicas = Y * X

    def moments(first_old, second_old, gradient):
        moment_one = beta_first * first_old + (1.0 - beta_first) * gradient
        moment_two = beta_second * second_old + (1.0 - beta_second) * gradient * gradient
        return moment_one, moment_two

    def pseudo_of(lo, width, gradient):
        at = slice(lo, lo + width)
        own_drift = drift[0, :, at]
        moment_one, moment_two = moments(adam_first[0, :, at], adam_second[0, :, at], gradient)
        update = moment_one / correction_one / (
            jnp.sqrt(moment_two / correction_two) + 1e-08
        ) + decay_weight * (anchor[:, at] + own_drift)
        pseudo = inner_rate * update - own_drift
        return pseudo.reshape(ROWS_DEV, replicas, width // replicas).transpose(1, 0, 2)

    def exchange(shares, axes=("y", "x")):
        return lax.all_to_all(shares, axes, split_axis=0, concat_axis=0, tiled=True)

    def finished(k, *tokens):
        moved = (lax.ppermute(up[k], "z", UP), lax.ppermute(down[k], "z", DOWN))
        u, d = after(moved, *tokens)
        return own(k, 0) + u + d

    half = finished(0, last)
    (_, early), (lo, late) = SHARES
    last = pseudo_of(0, early, half[:, :early])
    met = [exchange(last)]
    gradient = jnp.concatenate([half, finished(1, last, met)], axis=1)
    last = pseudo_of(lo, late, gradient[:, lo:])
    met.append(exchange(last))
    part = jnp.concatenate([jnp.sum(after(m, last), axis=0) / replicas for m in met], axis=1)
    pieces = exchange(jnp.broadcast_to(part[None], (replicas,) + part.shape))
    moment_one, moment_two = moments(adam_first[0], adam_second[0], gradient)
    squares = jnp.sum(jnp.sum(pieces * pieces, axis=(0, 1)).reshape(-1, 128), axis=0)
    squares = exchange(jnp.broadcast_to(squares, (PARTS, 1, 128)), ("z", "c"))
    momentum, updated = finish(squares, pieces, anchor, outer_momentum)
    return (moment_one[None], moment_two[None], momentum, updated)


def solution(mesh):
    devices = mesh.devices.reshape(Y, X, Z, C)
    grid = Mesh(devices, ("y", "x", "z", "c"))
    rep, fsdp = ("y", "x"), ("z", "c")
    return jax.shard_map(
        per_device,
        mesh=grid,
        in_specs=(
            P(rep, fsdp, None),
            P(rep, fsdp, None),
            P(fsdp, None),
            P(rep, fsdp, None),
            P(rep, fsdp, None),
            P(rep, fsdp, None),
            P(fsdp, None),
        ),
        out_specs=(
            P(rep, fsdp, None),
            P(rep, fsdp, None),
            P(fsdp, None),
            P(fsdp, None),
        ),
        check_vma=False,
    )
```

```python
import math

import jax
import jax.numpy as jnp
from jax import lax
from jax.experimental import pallas as pl
from jax.experimental.pallas import tpu as pltpu
from jax.sharding import Mesh, PartitionSpec as P

D = 8192
INNER_STEP = 100

beta_first = 0.9
beta_second = 0.95
inner_rate = 0.5
decay_weight = 0.1
outer_rate = 0.7
momentum_coef = 0.9

Y, X, Z, C = 4, 4, 8, 2
ROWS_DEV = 32
PARTS = Z * C
WIDTH = D // 2
CHUNKS = ((0, WIDTH), (WIDTH, WIDTH // 2), (WIDTH + WIDTH // 2, WIDTH // 2))
EARLY = ((0, 0), (1, 0), (0, 1), (1, 1), (0, 2), (2, 0), (0, 3), (2, 1), (1, 2))
STEPS = (4, 3, 5, 2, 6, 1, 7, 0)
UP = [(i, (i + 1) % Z) for i in range(Z)]
DOWN = [(i, (i - 1) % Z) for i in range(Z)]
SWAP = [(0, 1), (1, 0)]


def reorder_rows(activations, z, c):
    rows = Z * C * ROWS_DEV
    place = lax.broadcasted_iota(jnp.int32, (rows, rows), 1)
    source = lax.broadcasted_iota(jnp.int32, (rows, rows), 0)
    block = place // ROWS_DEV
    mine = jnp.where(block < 2, block == 1, block >= 2 + (Z - 1))
    slot = jnp.where(block < 2, 0, jnp.where(block < Z + 1, block - 1, block - Z))
    step = jnp.zeros_like(slot)
    for at, distance in enumerate(STEPS):
        step = jnp.where(slot == at, distance, step)
    core = jnp.where(mine, c, 1 - c)
    wanted = (((z + step) % Z) * C + core) * ROWS_DEV + place % ROWS_DEV
    pick = (wanted == source).astype(activations.dtype)
    return lax.dot_general(
        pick, activations, (((0,), (1,)), ((), ())), preferred_element_type=jnp.float32
    ).astype(activations.dtype)


def finish_kernel(squares_ref, pieces_ref, anchor_ref, momentum_ref, momentum_out, anchor_out):
    squares = jnp.sum(jnp.sum(squares_ref[...], axis=0), keepdims=True)
    ceiling = 0.3 * math.sqrt(ROWS_DEV * PARTS * D)
    factor = ceiling / jnp.maximum(jnp.sqrt(squares), ceiling)
    piece = pieces_ref.shape[2]
    for p in range(pieces_ref.shape[0]):
        at = slice(p * piece, (p + 1) * piece)
        scaled = factor * pieces_ref[p]
        momentum = momentum_coef * momentum_ref[:, at] + scaled
        momentum_out[:, at] = momentum
        anchor_out[:, at] = anchor_ref[:, at] - outer_rate * (scaled + momentum_coef * momentum)


def finish(squares, pieces, anchor, outer_momentum):
    replicas, _, both = pieces.shape
    part = pl.BlockSpec((ROWS_DEV, WIDTH), lambda h: (0, h))
    shape = jax.ShapeDtypeStruct(anchor.shape, jnp.float32)
    return pl.pallas_call(
        finish_kernel,
        grid=(2,),
        in_specs=[
            pl.BlockSpec(squares.shape, lambda h: (0, 0, 0)),
            pl.BlockSpec((replicas, ROWS_DEV, both // 2), lambda h: (0, 0, h)),
            part,
            part,
        ],
        out_specs=[part, part],
        out_shape=[shape, shape],
        cost_estimate=pl.CostEstimate(flops=7 * anchor.size, bytes_accessed=20 * anchor.size, transcendentals=0),
    )(squares, pieces, anchor, outer_momentum)


def per_device(hidden_acts, out_grads, anchor, drift, adam_first, adam_second, outer_momentum):
    z = lax.axis_index("z")
    c = lax.axis_index("c")
    ordered = reorder_rows(hidden_acts[0], z, c)
    cotangent = out_grads[0]
    near = 2 * ROWS_DEV
    stay = near + (Z - 1) * ROWS_DEV

    def product(lhs, rhs):
        return lax.dot_general(lhs, rhs, (((1,), (0,)), ((), ())), preferred_element_type=jnp.float32)

    def after(values, *tokens):
        return lax.optimization_barrier((values, tokens))[0]

    moved = [None] * len(CHUNKS)

    def own(k, distance, lo=0, hi=None):
        at = (STEPS.index(distance) - 1) * ROWS_DEV
        base, width = CHUNKS[k]
        hi = width if hi is None else hi
        return kept[k][at : at + ROWS_DEV, lo:hi] + rest[at : at + ROWS_DEV, base + lo : base + hi]

    def send(k, t, *tokens):
        lo, width = CHUNKS[k]
        half = width // 2
        if t == 0:
            source = after(first, *tokens)
            up, down = source[:, lo + half : lo + width], source[:, lo : lo + half]
        else:
            u, d = after(moved[k], *tokens)
            if t == 1:
                up = jnp.concatenate([own(k, 3, 0, half), own(k, 3, half) + u], axis=1)
                down = jnp.concatenate([own(k, 5, 0, half) + d, own(k, 5, half)], axis=1)
            else:
                up = own(k, 4 - t) + u
                down = own(k, 4 + t) + d
        moved[k] = (lax.ppermute(up, "z", UP), lax.ppermute(down, "z", DOWN))
        return up, down

    def finished(k, *tokens):
        u, d = after(moved[k], *tokens)
        return own(k, 0) + u + d

    first = product(ordered[:near], cotangent)
    theirs = lax.optimization_barrier(first[:ROWS_DEV])
    got = lax.ppermute(theirs, "c", SWAP)
    sent = product(after(ordered[near:stay], theirs), cotangent)
    rest = lax.ppermute(after(sent, got), "c", SWAP)
    first = first[ROWS_DEV:] + got
    last = ()
    for k, t in EARLY[:2]:
        last = send(k, t, last)
    lhs = after(ordered[stay:], sent, last)
    kept = [product(lhs, cotangent[:, lo : lo + width]) for lo, width in CHUNKS]
    for k, t in EARLY[2:]:
        last = send(k, t, last)

    correction_one = 1.0 - beta_first**INNER_STEP
    correction_two = 1.0 - beta_second**INNER_STEP
    replicas = Y * X
    piece = WIDTH // replicas

    def moments(first_old, second_old, gradient):
        moment_one = beta_first * first_old + (1.0 - beta_first) * gradient
        moment_two = beta_second * second_old + (1.0 - beta_second) * gradient * gradient
        return moment_one, moment_two

    def pseudo_of(lo, gradient):
        at = slice(lo, lo + WIDTH)
        own_drift = drift[0, :, at]
        moment_one, moment_two = moments(adam_first[0, :, at], adam_second[0, :, at], gradient)
        update = moment_one / correction_one / (
            jnp.sqrt(moment_two / correction_two) + 1e-08
        ) + decay_weight * (anchor[:, at] + own_drift)
        pseudo = inner_rate * update - own_drift
        return pseudo.reshape(ROWS_DEV, replicas, piece).transpose(1, 0, 2)

    def exchange(shares, axes=("y", "x")):
        return lax.all_to_all(shares, axes, split_axis=0, concat_axis=0, tiled=True)

    gradient_one = finished(0, last)
    last = pseudo_of(0, gradient_one)
    met = exchange(last)
    last = send(2, 2, last)
    last = send(1, 3, last)
    part = jnp.sum(after(met, last), axis=0)
    last = send(2, 3, last, part)
    gradient_two = finished(1, last)
    gradient_three = finished(2, gradient_two)
    gradient_two = jnp.concatenate([gradient_two, gradient_three], axis=1)
    met = exchange(pseudo_of(WIDTH, gradient_two))
    part = jnp.concatenate([part, jnp.sum(met, axis=0)], axis=1) / replicas
    pieces = exchange(jnp.broadcast_to(part[None], (replicas,) + part.shape))
    gradient = jnp.concatenate([gradient_one, gradient_two], axis=1)
    moment_one, moment_two = moments(adam_first[0], adam_second[0], gradient)
    squares = jnp.sum(jnp.sum(pieces * pieces, axis=(0, 1)).reshape(-1, 128), axis=0)
    squares = exchange(jnp.broadcast_to(squares, (PARTS, 1, 128)), ("z", "c"))
    momentum, updated = finish(squares, pieces, anchor, outer_momentum)
    return (moment_one[None], moment_two[None], momentum, updated)


def solution(mesh):
    devices = mesh.devices.reshape(Y, X, Z, C)
    grid = Mesh(devices, ("y", "x", "z", "c"))
    rep, fsdp = ("y", "x"), ("z", "c")
    return jax.shard_map(
        per_device,
        mesh=grid,
        in_specs=(
            P(rep, fsdp, None),
            P(rep, fsdp, None),
            P(fsdp, None),
            P(rep, fsdp, None),
            P(rep, fsdp, None),
            P(rep, fsdp, None),
            P(fsdp, None),
        ),
        out_specs=(
            P(rep, fsdp, None),
            P(rep, fsdp, None),
            P(fsdp, None),
            P(fsdp, None),
        ),
        check_vma=False,
    )
```

```python
import math

import jax
import jax.numpy as jnp
from jax import lax
from jax.experimental import pallas as pl
from jax.experimental.pallas import tpu as pltpu
from jax.sharding import Mesh, PartitionSpec as P

D = 8192
INNER_STEP = 100

beta_first = 0.9
beta_second = 0.95
inner_rate = 0.5
decay_weight = 0.1
outer_rate = 0.7
momentum_coef = 0.9

Y, X, Z, C = 4, 4, 8, 2
ROWS_DEV = 32
PARTS = Z * C
CHUNKS = 2
WIDTH = D // CHUNKS
HALF = WIDTH // 2
STEPS = (4, 3, 5, 2, 6, 1, 7, 0)
UP = [(i, (i + 1) % Z) for i in range(Z)]
DOWN = [(i, (i - 1) % Z) for i in range(Z)]
SWAP = [(0, 1), (1, 0)]


def reorder_rows(activations, z, c):
    rows = Z * C * ROWS_DEV
    place = lax.broadcasted_iota(jnp.int32, (rows, rows), 1)
    source = lax.broadcasted_iota(jnp.int32, (rows, rows), 0)
    block = place // ROWS_DEV
    mine = jnp.where(block < 2, block == 1, block >= 2 + (Z - 1))
    slot = jnp.where(block < 2, 0, jnp.where(block < Z + 1, block - 1, block - Z))
    step = jnp.zeros_like(slot)
    for at, distance in enumerate(STEPS):
        step = jnp.where(slot == at, distance, step)
    core = jnp.where(mine, c, 1 - c)
    wanted = (((z + step) % Z) * C + core) * ROWS_DEV + place % ROWS_DEV
    pick = (wanted == source).astype(activations.dtype)
    return lax.dot_general(
        pick, activations, (((0,), (1,)), ((), ())), preferred_element_type=jnp.float32
    ).astype(activations.dtype)


def finish_kernel(squares_ref, pieces_ref, anchor_ref, momentum_ref, momentum_out, anchor_out):
    squares = jnp.sum(jnp.sum(squares_ref[...], axis=0), keepdims=True)
    ceiling = 0.3 * math.sqrt(ROWS_DEV * PARTS * D)
    factor = ceiling / jnp.maximum(jnp.sqrt(squares), ceiling)
    piece = pieces_ref.shape[2]
    for p in range(pieces_ref.shape[0]):
        at = slice(p * piece, (p + 1) * piece)
        scaled = factor * pieces_ref[p]
        momentum = momentum_coef * momentum_ref[:, at] + scaled
        momentum_out[:, at] = momentum
        anchor_out[:, at] = anchor_ref[:, at] - outer_rate * (scaled + momentum_coef * momentum)


def finish(squares, pieces, anchor, outer_momentum):
    replicas, _, both = pieces.shape
    blocks = 2
    part = pl.BlockSpec((ROWS_DEV, WIDTH // blocks), lambda h, q: (0, h * blocks + q))
    shape = jax.ShapeDtypeStruct(anchor.shape, jnp.float32)
    return pl.pallas_call(
        finish_kernel,
        grid=(CHUNKS, blocks),
        in_specs=[
            pl.BlockSpec(squares.shape, lambda h, q: (0, 0, 0)),
            pl.BlockSpec((replicas // blocks, ROWS_DEV, both // CHUNKS), lambda h, q: (q, 0, h)),
            part,
            part,
        ],
        out_specs=[part, part],
        out_shape=[shape, shape],
        cost_estimate=pl.CostEstimate(flops=7 * anchor.size, bytes_accessed=20 * anchor.size, transcendentals=0),
    )(squares, pieces, anchor, outer_momentum)


def per_device(hidden_acts, out_grads, anchor, drift, adam_first, adam_second, outer_momentum):
    z = lax.axis_index("z")
    c = lax.axis_index("c")
    ordered = reorder_rows(hidden_acts[0], z, c)
    cotangent = out_grads[0]
    near = 2 * ROWS_DEV
    stay = near + (Z - 1) * ROWS_DEV

    def product(lhs, rhs):
        return lax.dot_general(lhs, rhs, (((1,), (0,)), ((), ())), preferred_element_type=jnp.float32)

    def after(values, *tokens):
        return lax.optimization_barrier((values, tokens))[0]

    chunks = range(CHUNKS)
    cols = [lax.slice_in_dim(cotangent, k * WIDTH, (k + 1) * WIDTH, axis=1) for k in chunks]
    up = [None] * CHUNKS
    down = [None] * CHUNKS

    def own(k, distance, lo=0, hi=WIDTH):
        at = (STEPS.index(distance) - 1) * ROWS_DEV
        base = k * WIDTH
        return kept[k][at : at + ROWS_DEV, lo:hi] + rest[at : at + ROWS_DEV, base + lo : base + hi]

    first = product(ordered[:near], cotangent)
    theirs = lax.optimization_barrier(first[:ROWS_DEV])
    got = lax.ppermute(theirs, "c", SWAP)
    sent = product(after(ordered[near:stay], theirs), cotangent)
    rest = lax.ppermute(after(sent, got), "c", SWAP)
    first = first[ROWS_DEV:] + got
    for k in chunks:
        up[k] = first[:, k * WIDTH + HALF : (k + 1) * WIDTH]
        down[k] = first[:, k * WIDTH : k * WIDTH + HALF]
        first = after(first, up[k], down[k])
    last = (up[-1], down[-1])
    lhs = after(ordered[stay:], sent, last)
    kept = [product(lhs, cols[k]) for k in chunks]
    for t in range(1, 4):
        for k in chunks:
            moved = (lax.ppermute(up[k], "z", UP), lax.ppermute(down[k], "z", DOWN))
            u, d = after(moved, last)
            if t == 1:
                up[k] = jnp.concatenate([own(k, 3, 0, HALF), own(k, 3, HALF, WIDTH) + u], axis=1)
                down[k] = jnp.concatenate([own(k, 5, 0, HALF) + d, own(k, 5, HALF, WIDTH)], axis=1)
            else:
                up[k] = own(k, 4 - t) + u
                down[k] = own(k, 4 + t) + d
            last = (up[k], down[k])

    correction_one = 1.0 - beta_first**INNER_STEP
    correction_two = 1.0 - beta_second**INNER_STEP
    replicas = Y * X
    piece = WIDTH // replicas

    def moments(first_old, second_old, gradient):
        moment_one = beta_first * first_old + (1.0 - beta_first) * gradient
        moment_two = beta_second * second_old + (1.0 - beta_second) * gradient * gradient
        return moment_one, moment_two

    def pseudo_of(k, gradient):
        at = slice(k * WIDTH, (k + 1) * WIDTH)
        own_drift = drift[0, :, at]
        moment_one, moment_two = moments(adam_first[0, :, at], adam_second[0, :, at], gradient)
        update = moment_one / correction_one / (
            jnp.sqrt(moment_two / correction_two) + 1e-08
        ) + decay_weight * (anchor[:, at] + own_drift)
        pseudo = inner_rate * update - own_drift
        return pseudo.reshape(ROWS_DEV, replicas, piece).transpose(1, 0, 2)

    gradients = []
    spread = []
    for k in chunks:
        moved = (lax.ppermute(up[k], "z", UP), lax.ppermute(down[k], "z", DOWN))
        u, d = after(moved, last, spread)
        gradients.append(own(k, 0) + u + d)
        spread.append(pseudo_of(k, gradients[k]))
    moment_one, moment_two = moments(adam_first[0], adam_second[0], jnp.concatenate(gradients, axis=1))
    spread = jnp.concatenate(spread, axis=2)
    met = lax.all_to_all(spread, ("y", "x"), split_axis=0, concat_axis=0, tiled=True)
    part = jnp.sum(met, axis=0) / replicas
    copies = jnp.broadcast_to(part[None], (replicas,) + part.shape)
    pieces = lax.all_to_all(copies, ("y", "x"), split_axis=0, concat_axis=0, tiled=True)
    squares = jnp.sum(jnp.sum(pieces * pieces, axis=(0, 1)).reshape(-1, 128), axis=0)
    squares = jnp.broadcast_to(squares, (PARTS, 1, 128))
    squares = lax.all_to_all(squares, ("z", "c"), split_axis=0, concat_axis=0, tiled=True)
    momentum, updated = finish(squares, pieces, anchor, outer_momentum)
    return (moment_one[None], moment_two[None], momentum, updated)


def solution(mesh):
    devices = mesh.devices.reshape(Y, X, Z, C)
    grid = Mesh(devices, ("y", "x", "z", "c"))
    rep, fsdp = ("y", "x"), ("z", "c")
    return jax.shard_map(
        per_device,
        mesh=grid,
        in_specs=(
            P(rep, fsdp, None),
            P(rep, fsdp, None),
            P(fsdp, None),
            P(rep, fsdp, None),
            P(rep, fsdp, None),
            P(rep, fsdp, None),
            P(fsdp, None),
        ),
        out_specs=(
            P(rep, fsdp, None),
            P(rep, fsdp, None),
            P(fsdp, None),
            P(fsdp, None),
        ),
        check_vma=False,
    )
```

```python
import math

import jax
import jax.numpy as jnp
from jax import lax
from jax.experimental import pallas as pl
from jax.experimental.pallas import tpu as pltpu
from jax.sharding import Mesh, PartitionSpec as P

D = 8192
INNER_STEP = 100

beta_first = 0.9
beta_second = 0.95
inner_rate = 0.5
decay_weight = 0.1
outer_rate = 0.7
momentum_coef = 0.9

Y, X, Z, C = 4, 4, 8, 2
ROWS_DEV = 32
PARTS = Z * C
CHUNKS = 2
WIDTH = D // CHUNKS
HALF = WIDTH // 2
STEPS = (4, 3, 5, 2, 6, 1, 7, 0)
UP = [(i, (i + 1) % Z) for i in range(Z)]
DOWN = [(i, (i - 1) % Z) for i in range(Z)]
SWAP = [(0, 1), (1, 0)]


def reorder_rows(activations, z, c):
    rows = Z * C * ROWS_DEV
    place = lax.broadcasted_iota(jnp.int32, (rows, rows), 1)
    source = lax.broadcasted_iota(jnp.int32, (rows, rows), 0)
    block = place // ROWS_DEV
    mine = jnp.where(block < 2, block == 1, block >= 2 + (Z - 1))
    slot = jnp.where(block < 2, 0, jnp.where(block < Z + 1, block - 1, block - Z))
    step = jnp.zeros_like(slot)
    for at, distance in enumerate(STEPS):
        step = jnp.where(slot == at, distance, step)
    core = jnp.where(mine, c, 1 - c)
    wanted = (((z + step) % Z) * C + core) * ROWS_DEV + place % ROWS_DEV
    pick = (wanted == source).astype(activations.dtype)
    return lax.dot_general(
        pick, activations, (((0,), (1,)), ((), ())), preferred_element_type=jnp.float32
    ).astype(activations.dtype)


def finish_kernel(squares_ref, pieces_ref, anchor_ref, momentum_ref, momentum_out, anchor_out):
    squares = jnp.sum(jnp.sum(squares_ref[...], axis=0), keepdims=True)
    ceiling = 0.3 * math.sqrt(ROWS_DEV * PARTS * D)
    factor = ceiling / jnp.maximum(jnp.sqrt(squares), ceiling)
    piece = pieces_ref.shape[2]
    for p in range(pieces_ref.shape[0]):
        at = slice(p * piece, (p + 1) * piece)
        scaled = factor * pieces_ref[p]
        momentum = momentum_coef * momentum_ref[:, at] + scaled
        momentum_out[:, at] = momentum
        anchor_out[:, at] = anchor_ref[:, at] - outer_rate * (scaled + momentum_coef * momentum)


def finish(squares, pieces, anchor, outer_momentum):
    replicas, _, piece = pieces.shape
    parts = 2
    part = pl.BlockSpec((ROWS_DEV, D // parts), lambda h: (0, h))
    shape = jax.ShapeDtypeStruct(anchor.shape, jnp.float32)
    return pl.pallas_call(
        finish_kernel,
        grid=(parts,),
        in_specs=[
            pl.BlockSpec(squares.shape, lambda h: (0, 0, 0)),
            pl.BlockSpec((replicas // parts, ROWS_DEV, piece), lambda h: (h, 0, 0)),
            part,
            part,
        ],
        out_specs=[part, part],
        out_shape=[shape, shape],
        cost_estimate=pl.CostEstimate(flops=7 * anchor.size, bytes_accessed=20 * anchor.size, transcendentals=0),
    )(squares, pieces, anchor, outer_momentum)


def per_device(hidden_acts, out_grads, anchor, drift, adam_first, adam_second, outer_momentum):
    z = lax.axis_index("z")
    c = lax.axis_index("c")
    ordered = reorder_rows(hidden_acts[0], z, c)
    cotangent = out_grads[0]
    near = 2 * ROWS_DEV
    stay = near + (Z - 1) * ROWS_DEV

    def product(lhs, rhs):
        return lax.dot_general(lhs, rhs, (((1,), (0,)), ((), ())), preferred_element_type=jnp.float32)

    def after(values, *tokens):
        return lax.optimization_barrier((values, tokens))[0]

    chunks = range(CHUNKS)
    cols = [lax.slice_in_dim(cotangent, k * WIDTH, (k + 1) * WIDTH, axis=1) for k in chunks]
    up = [None] * CHUNKS
    down = [None] * CHUNKS

    def own(k, distance, lo=0, hi=WIDTH):
        at = (STEPS.index(distance) - 1) * ROWS_DEV
        base = k * WIDTH
        return kept[k][at : at + ROWS_DEV, lo:hi] + rest[at : at + ROWS_DEV, base + lo : base + hi]

    first = product(ordered[:near], cotangent)
    theirs = lax.optimization_barrier(first[:ROWS_DEV])
    got = lax.ppermute(theirs, "c", SWAP)
    sent = product(after(ordered[near:stay], theirs), cotangent)
    rest = lax.ppermute(after(sent, got), "c", SWAP)
    first = first[ROWS_DEV:] + got
    for k in chunks:
        up[k] = first[:, k * WIDTH + HALF : (k + 1) * WIDTH]
        down[k] = first[:, k * WIDTH : k * WIDTH + HALF]
        first = after(first, up[k], down[k])
    last = (up[-1], down[-1])
    lhs = after(ordered[stay:], sent, last)
    kept = [product(lhs, cols[k]) for k in chunks]
    for t in range(1, 5):
        for k in chunks:
            moved = (lax.ppermute(up[k], "z", UP), lax.ppermute(down[k], "z", DOWN))
            u, d = after(moved, last)
            if t == 1:
                up[k] = jnp.concatenate([own(k, 3, 0, HALF), own(k, 3, HALF, WIDTH) + u], axis=1)
                down[k] = jnp.concatenate([own(k, 5, 0, HALF) + d, own(k, 5, HALF, WIDTH)], axis=1)
            elif t < 4:
                up[k] = own(k, 4 - t) + u
                down[k] = own(k, 4 + t) + d
            else:
                up[k] = down[k] = own(k, 0) + u + d
            last = (up[k], down[k])

    gradient = jnp.concatenate(up, axis=1)
    correction_one = 1.0 - beta_first**INNER_STEP
    correction_two = 1.0 - beta_second**INNER_STEP
    own_drift = drift[0]
    moment_one = beta_first * adam_first[0] + (1.0 - beta_first) * gradient
    moment_two = beta_second * adam_second[0] + (1.0 - beta_second) * gradient * gradient
    update = moment_one / correction_one / (
        jnp.sqrt(moment_two / correction_two) + 1e-08
    ) + decay_weight * (anchor + own_drift)
    pseudo = inner_rate * update - own_drift

    replicas = Y * X
    piece = D // replicas
    spread = pseudo.reshape(ROWS_DEV, replicas, piece).transpose(1, 0, 2)
    met = lax.all_to_all(spread, ("y", "x"), split_axis=0, concat_axis=0, tiled=True)
    gradient = after(gradient, spread)
    moment_one = beta_first * adam_first[0] + (1.0 - beta_first) * gradient
    moment_two = beta_second * adam_second[0] + (1.0 - beta_second) * gradient * gradient
    moment_one, moment_two, met = lax.optimization_barrier((moment_one, moment_two, met))
    part = jnp.sum(met, axis=0) / replicas
    copies = jnp.broadcast_to(part[None], (replicas, ROWS_DEV, piece))
    pieces = lax.all_to_all(copies, ("y", "x"), split_axis=0, concat_axis=0, tiled=True)
    squares = jnp.sum(jnp.sum(pieces * pieces, axis=(0, 1)).reshape(-1, 128), axis=0)
    squares = jnp.broadcast_to(squares, (PARTS, 1, 128))
    squares = lax.all_to_all(squares, ("z", "c"), split_axis=0, concat_axis=0, tiled=True)
    momentum, updated = finish(squares, pieces, anchor, outer_momentum)
    return (moment_one[None], moment_two[None], momentum, updated)


def solution(mesh):
    devices = mesh.devices.reshape(Y, X, Z, C)
    grid = Mesh(devices, ("y", "x", "z", "c"))
    rep, fsdp = ("y", "x"), ("z", "c")
    return jax.shard_map(
        per_device,
        mesh=grid,
        in_specs=(
            P(rep, fsdp, None),
            P(rep, fsdp, None),
            P(fsdp, None),
            P(rep, fsdp, None),
            P(rep, fsdp, None),
            P(rep, fsdp, None),
            P(fsdp, None),
        ),
        out_specs=(
            P(rep, fsdp, None),
            P(rep, fsdp, None),
            P(fsdp, None),
            P(fsdp, None),
        ),
        check_vma=False,
    )
```

```python
import math

import jax
import jax.numpy as jnp
from jax import lax
from jax.experimental import pallas as pl
from jax.experimental.pallas import tpu as pltpu
from jax.sharding import Mesh, PartitionSpec as P

D = 8192
INNER_STEP = 100

beta_first = 0.9
beta_second = 0.95
inner_rate = 0.5
decay_weight = 0.1
outer_rate = 0.7
momentum_coef = 0.9

Y, X, Z, C = 4, 4, 8, 2
ROWS_DEV = 32
PARTS = Z * C
CHUNKS = 2
WIDTH = D // CHUNKS
HALF = WIDTH // 2
STEPS = (4, 3, 5, 2, 6, 1, 7, 0)
UP = [(i, (i + 1) % Z) for i in range(Z)]
DOWN = [(i, (i - 1) % Z) for i in range(Z)]
SWAP = [(0, 1), (1, 0)]


def reorder_rows(activations, z, c):
    rows = Z * C * ROWS_DEV
    place = lax.broadcasted_iota(jnp.int32, (rows, rows), 1)
    source = lax.broadcasted_iota(jnp.int32, (rows, rows), 0)
    block = place // ROWS_DEV
    mine = jnp.where(block < 2, block == 1, block >= 2 + (Z - 1))
    slot = jnp.where(block < 2, 0, jnp.where(block < Z + 1, block - 1, block - Z))
    step = jnp.zeros_like(slot)
    for at, distance in enumerate(STEPS):
        step = jnp.where(slot == at, distance, step)
    core = jnp.where(mine, c, 1 - c)
    wanted = (((z + step) % Z) * C + core) * ROWS_DEV + place % ROWS_DEV
    pick = (wanted == source).astype(activations.dtype)
    return lax.dot_general(
        pick, activations, (((0,), (1,)), ((), ())), preferred_element_type=jnp.float32
    ).astype(activations.dtype)


def finish_kernel(squares_ref, pieces_ref, anchor_ref, momentum_ref, momentum_out, anchor_out):
    squares = jnp.sum(jnp.sum(squares_ref[...], axis=0), keepdims=True)
    ceiling = 0.3 * math.sqrt(ROWS_DEV * PARTS * D)
    factor = ceiling / jnp.maximum(jnp.sqrt(squares), ceiling)
    piece = pieces_ref.shape[2]
    for p in range(pieces_ref.shape[0]):
        at = slice(p * piece, (p + 1) * piece)
        scaled = factor * pieces_ref[p]
        momentum = momentum_coef * momentum_ref[:, at] + scaled
        momentum_out[:, at] = momentum
        anchor_out[:, at] = anchor_ref[:, at] - outer_rate * (scaled + momentum_coef * momentum)


def finish(squares, pieces, anchor, outer_momentum):
    replicas, _, piece = pieces.shape
    parts = 1
    part = pl.BlockSpec((ROWS_DEV, D // parts), lambda h: (0, h))
    shape = jax.ShapeDtypeStruct(anchor.shape, jnp.float32)
    return pl.pallas_call(
        finish_kernel,
        grid=(parts,),
        in_specs=[
            pl.BlockSpec(squares.shape, lambda h: (0, 0, 0)),
            pl.BlockSpec((replicas // parts, ROWS_DEV, piece), lambda h: (h, 0, 0)),
            part,
            part,
        ],
        out_specs=[part, part],
        out_shape=[shape, shape],
        cost_estimate=pl.CostEstimate(flops=7 * anchor.size, bytes_accessed=20 * anchor.size, transcendentals=0),
    )(squares, pieces, anchor, outer_momentum)


def per_device(hidden_acts, out_grads, anchor, drift, adam_first, adam_second, outer_momentum):
    z = lax.axis_index("z")
    c = lax.axis_index("c")
    ordered = reorder_rows(hidden_acts[0], z, c)
    cotangent = out_grads[0]
    near = 2 * ROWS_DEV
    stay = near + (Z - 1) * ROWS_DEV

    def product(lhs, rhs):
        return lax.dot_general(lhs, rhs, (((1,), (0,)), ((), ())), preferred_element_type=jnp.float32)

    def after(values, *tokens):
        return lax.optimization_barrier((values, tokens))[0]

    chunks = range(CHUNKS)
    cols = [lax.slice_in_dim(cotangent, k * WIDTH, (k + 1) * WIDTH, axis=1) for k in chunks]
    up = [None] * CHUNKS
    down = [None] * CHUNKS

    def own(k, distance, lo=0, hi=WIDTH):
        at = (STEPS.index(distance) - 1) * ROWS_DEV
        base = k * WIDTH
        return kept[k][at : at + ROWS_DEV, lo:hi] + rest[at : at + ROWS_DEV, base + lo : base + hi]

    first = product(ordered[:near], cotangent)
    theirs = lax.optimization_barrier(first[:ROWS_DEV])
    got = lax.ppermute(theirs, "c", SWAP)
    sent = product(after(ordered[near:stay], theirs), cotangent)
    rest = lax.ppermute(after(sent, got), "c", SWAP)
    first = first[ROWS_DEV:] + got
    for k in chunks:
        up[k] = first[:, k * WIDTH + HALF : (k + 1) * WIDTH]
        down[k] = first[:, k * WIDTH : k * WIDTH + HALF]
        first = after(first, up[k], down[k])
    last = (up[-1], down[-1])
    lhs = after(ordered[stay:], sent, last)
    kept = [product(lhs, cols[k]) for k in chunks]
    for t in range(1, 5):
        for k in chunks:
            moved = (lax.ppermute(up[k], "z", UP), lax.ppermute(down[k], "z", DOWN))
            u, d = after(moved, last)
            if t == 1:
                up[k] = jnp.concatenate([own(k, 3, 0, HALF), own(k, 3, HALF, WIDTH) + u], axis=1)
                down[k] = jnp.concatenate([own(k, 5, 0, HALF) + d, own(k, 5, HALF, WIDTH)], axis=1)
            elif t < 4:
                up[k] = own(k, 4 - t) + u
                down[k] = own(k, 4 + t) + d
            else:
                up[k] = down[k] = own(k, 0) + u + d
            last = (up[k], down[k])

    gradient = jnp.concatenate(up, axis=1)
    correction_one = 1.0 - beta_first**INNER_STEP
    correction_two = 1.0 - beta_second**INNER_STEP
    own_drift = drift[0]
    moment_one = beta_first * adam_first[0] + (1.0 - beta_first) * gradient
    moment_two = beta_second * adam_second[0] + (1.0 - beta_second) * gradient * gradient
    update = moment_one / correction_one / (
        jnp.sqrt(moment_two / correction_two) + 1e-08
    ) + decay_weight * (anchor + own_drift)
    pseudo = inner_rate * update - own_drift

    replicas = Y * X
    piece = D // replicas
    spread = pseudo.reshape(ROWS_DEV, replicas, piece).transpose(1, 0, 2)
    met = lax.all_to_all(spread, ("y", "x"), split_axis=0, concat_axis=0, tiled=True)
    part = jnp.sum(met, axis=0) / replicas
    copies = jnp.broadcast_to(part[None], (replicas, ROWS_DEV, piece))
    pieces = lax.all_to_all(copies, ("y", "x"), split_axis=0, concat_axis=0, tiled=True)
    squares = jnp.sum(jnp.sum(pieces * pieces, axis=(0, 1)).reshape(-1, 128), axis=0)
    squares = jnp.broadcast_to(squares, (PARTS, 1, 128))
    squares = lax.all_to_all(squares, ("z", "c"), split_axis=0, concat_axis=0, tiled=True)
    momentum, updated = finish(squares, pieces, anchor, outer_momentum)
    return (moment_one[None], moment_two[None], momentum, updated)


def solution(mesh):
    devices = mesh.devices.reshape(Y, X, Z, C)
    grid = Mesh(devices, ("y", "x", "z", "c"))
    rep, fsdp = ("y", "x"), ("z", "c")
    return jax.shard_map(
        per_device,
        mesh=grid,
        in_specs=(
            P(rep, fsdp, None),
            P(rep, fsdp, None),
            P(fsdp, None),
            P(rep, fsdp, None),
            P(rep, fsdp, None),
            P(rep, fsdp, None),
            P(fsdp, None),
        ),
        out_specs=(
            P(rep, fsdp, None),
            P(rep, fsdp, None),
            P(fsdp, None),
            P(fsdp, None),
        ),
        check_vma=False,
    )
```
